32 devices in a mesh: trial: 16 (over z, y, x), factor: 2 (over core).
Axes of the slice: x: 2, y: 2, z: 4, core: 2. Of those that a mesh axis runs over, the one named last changes fastest.
Arguments:
- observed: float32 [64, 32, 128], P('trial'), may hold values from -6 to 6
- trial_mean: float32 [64], P('trial'), may hold values from -4 to 4
- correlations: float32 [64, 2], P('trial'), may hold values from 0.1 to 0.7
- noise_var: float32 [64], P('trial'), may hold values from 2 to 8
- plot_slot: int32 [64, 32, 128], P('trial'), may hold values from 0 to 2047
- row_count: int32 [64], P('trial'), may hold values from 8 to 32, as said below
- col_count: int32 [64], P('trial'), may hold values from 64 to 128, as said below
- panel_list: int32 [64, 16], P('trial'), may hold values from 0 to 191, as said below
- scores: bfloat16 [128, 24576], P('factor', 'trial'), may hold values from -0.5 to 0.5
- loadings: float32 [64, 128], P('trial', 'factor'), may hold values from -5 to 5
- score_precision: float32 [128], P('factor'), may hold values from 20 to 80
Outputs:
- score_gradient: float32 [128, 24576], P('factor', 'trial')
- loading_gradient: float32 [64, 128], P('trial', 'factor')
The draws below stay inside these ranges and needn't reach their ends.
Inputs may be any that keep to these rules, and one draw needn't show every extreme that they name: `panel_list`: panel p is owned by index p // 12 of trial. Among the 64 entries of each aligned block of 4 trials, no owner holds more than 8 of them, and in every block some owner holds exactly that many. Entries may repeat. `row_count`: the first trial uses all 32 rows. `col_count`: the first trial uses all 128 columns.
All inputs are finite; a program needn't handle non-finite values.
Results may differ from the reference program's by a relative error of at most 0.0023.
Values may be sent and summed in bfloat16 or wider, within the bound.
A program may use at most 64 MiB of HBM per device.

```python
import math
import jax
import jax.numpy as jnp
from jax import lax

K = 128
PANEL = 128
PT = 16
ROWS = 32
COLS = 128
TRIALS_DEV = 4
PANELS_DEV = 12
TRIALS = 64
PANELS = 192
GENOTYPES = 24576


def draw_row_count(key, part):
    lowest = max(2, ROWS // 4)
    values = jax.random.randint(jax.random.fold_in(key, 11), (TRIALS,), lowest, ROWS + 1)
    return values.at[0].set(ROWS).astype(jnp.int32)


def draw_col_count(key, part):
    lowest = max(2, COLS // 2)
    values = jax.random.randint(jax.random.fold_in(key, 12), (TRIALS,), lowest, COLS + 1)
    return values.at[0].set(COLS).astype(jnp.int32)


def draw_panel_list(key, part):
    owners_total = PANELS // PANELS_DEV
    required_count = TRIALS_DEV * PT
    most_count = 2 * required_count // owners_total
    quarter = owners_total // 4
    half_count = required_count // 2
    blocks = TRIALS // TRIALS_DEV

    def one_block(block_key):
        key_owner, key_sorted_order, key_local = jax.random.split(block_key, 3)
        shuffled = jax.random.permutation(key_owner, owners_total)
        places = jnp.arange(required_count)
        first_half = shuffled[jnp.minimum(places // most_count, owners_total - 1)]
        second_half = shuffled[quarter + (places - half_count) % (owners_total - quarter)]
        owner_ids = jnp.where(places < half_count, first_half, second_half)
        owner_ids = owner_ids[jax.random.permutation(key_sorted_order, required_count)]
        local_ids = jax.random.randint(key_local, (required_count,), 0, PANELS_DEV)
        return (owner_ids * PANELS_DEV + local_ids).reshape(TRIALS_DEV, PT)
    block_keys = jax.random.split(jax.random.fold_in(key, 7), blocks)
    return jax.vmap(one_block)(block_keys).reshape(TRIALS, PT).astype(jnp.int32)


def with_ends(values, own_key, low, largest):
    extent = values.shape
    index_at = [jax.random.randint(jax.random.fold_in(own_key, axis), (), 0, extent[axis]) for axis in range(len(extent))]
    values = values.at[tuple(index_at)].set(low)
    longest = extent.index(max(extent))
    index_at[longest] = (index_at[longest] + 1) % extent[longest]
    return values.at[tuple(index_at)].set(largest)


def levels(rng, dims, shards, least, largest):
    factor_of, own = 1.0, jax.random.fold_in(rng, 6)
    for dim, parts in shards:
        steps = jnp.exp(jax.random.uniform(jax.random.fold_in(own, dim), (parts,), jnp.float32, least / len(shards), largest / len(shards)))
        factor_of = factor_of * jnp.repeat(steps, dims[dim] // parts).reshape([-1 if axis == dim else 1 for axis in range(len(dims))])
    return factor_of


def scatter_about(stream_key, shape, spread, most, cuts=(), held_as=jnp.bfloat16):
    values = jax.random.normal(stream_key, shape, jnp.float32) * spread
    if len(cuts) > 0:
        values = levels(stream_key, shape, cuts, -0.22, 0.18) * values
    return jnp.clip(values, min=-most, max=most).astype(held_as)


def setup_inputs(seed: int = 0) -> dict:
    arg_keys = jax.random.split(jax.random.key(seed), 12)
    observed = scatter_about(arg_keys[0], (TRIALS, ROWS, COLS), 1.0, 6.0, ((0, 16),), jnp.float32)
    trial_mean = scatter_about(arg_keys[1], (TRIALS,), 1.0, 4.0, ((0, 16),), jnp.float32)
    correlations = jnp.clip(0.1 + 0.59999999 * jax.random.uniform(arg_keys[2], (TRIALS, 2), jnp.float32) ** levels(arg_keys[2], (TRIALS, 2), ((0, 16),), -0.2, 0.2), 0.1, 0.7)
    noise_var = jnp.clip(jnp.exp(math.log(8.0) - 1.3862944 * jax.random.uniform(arg_keys[3], (TRIALS,), jnp.float32) ** levels(arg_keys[3], (TRIALS,), ((0, 16),), -0.2, 0.2)), 2.0, 8.0)
    plot_slot = with_ends(jax.random.randint(arg_keys[4], (TRIALS, ROWS, COLS), 0, PT * PANEL), jax.random.fold_in(arg_keys[4], 1), 0, (PT * PANEL) - 1).astype(jnp.int32)
    row_count = draw_row_count(jax.random.fold_in(arg_keys[11], 71), 0)
    col_count = draw_col_count(jax.random.fold_in(arg_keys[11], 71), 0)
    panel_list = draw_panel_list(jax.random.fold_in(arg_keys[11], 71), 0)
    scores = scatter_about(arg_keys[8], (K, GENOTYPES), K ** -0.5, 0.5, ((0, 2), (1, 16)))
    loadings = scatter_about(arg_keys[9], (TRIALS, K), 1.0, 5.0, ((0, 16), (1, 2)), jnp.float32)
    score_precision = jnp.clip(jnp.exp(math.log(80.0) - 1.3862944 * jax.random.uniform(arg_keys[10], (K,), jnp.float32) ** levels(arg_keys[10], (K,), ((0, 2),), -0.2, 0.2)), 20.0, 80.0)
    return dict(observed=observed, trial_mean=trial_mean, correlations=correlations, noise_var=noise_var, plot_slot=plot_slot, row_count=row_count, col_count=col_count, panel_list=panel_list, scores=scores, loadings=loadings, score_precision=score_precision)


def sweep_axis(values_in, corr_value, position, limit_count, axis_number):
    factor_scale = 1.0 / (1.0 - corr_value * corr_value)
    interior = ((position > 0) & (position < limit_count - 1)).astype(values_in.dtype)
    padding = [(0, 0)] * values_in.ndim
    padding[axis_number] = (1, 1)
    padded = jnp.pad(values_in, padding)
    length = values_in.shape[axis_number]
    lower_side = lax.slice_in_dim(padded, 0, length, axis=axis_number)
    upper_side = lax.slice_in_dim(padded, 2, length + 2, axis=axis_number)
    result = factor_scale * ((1.0 + corr_value * corr_value * interior) * values_in - corr_value * (lower_side + upper_side))
    return jnp.where(position < limit_count, result, 0.0)


def evaluate(current, loads_all, observed, trial_mean, correlations, noise_var, plot_slot, row_count, col_count, panel_list, score_precision):
    grouped = current.reshape(K, PANELS, PANEL)
    row_index = lax.broadcasted_iota(jnp.int32, (ROWS, COLS), 0)
    col_index = lax.broadcasted_iota(jnp.int32, (ROWS, COLS), 1)

    def per_trial(accum, inputs):
        ids, loads_now, obs_grid, mean_value, corr_pair, noise_value, slot_grid, row_upper_limit, col_limit = inputs
        table = jnp.take(grouped, ids, axis=1).reshape(K, PT * PANEL).astype(jnp.float32)
        effect = jnp.dot(loads_now, table, precision=lax.Precision.HIGHEST)
        fitted = effect[slot_grid]
        active = (row_index < row_upper_limit) & (col_index < col_limit)
        residual = jnp.where(active, obs_grid - mean_value - fitted, 0.0)
        across = sweep_axis(residual, corr_pair[1], col_index, col_limit, 1)
        weighted = sweep_axis(across, corr_pair[0], row_index, row_upper_limit, 0) / noise_value
        slot_weight = jax.ops.segment_sum(weighted.reshape(-1), slot_grid.reshape(-1), num_segments=PT * PANEL)
        load_grad = -jnp.dot(table, slot_weight, precision=lax.Precision.HIGHEST)
        returned = -(loads_now[:, None] * slot_weight[None, :]).reshape(K, PT, PANEL)
        accum = accum.at[:, ids, :].add(returned)
        return accum, load_grad

    accum, load_grads = lax.scan(per_trial, jnp.zeros((K, PANELS, PANEL), jnp.float32),
                                 (panel_list, loads_all, observed, trial_mean, correlations, noise_var, plot_slot, row_count, col_count))
    score_grad = score_precision[:, None] * current.astype(jnp.float32) + accum.reshape(K, PANELS * PANEL)
    return score_grad, load_grads


def reference(observed, trial_mean, correlations, noise_var, plot_slot, row_count, col_count, panel_list, scores, loadings, score_precision):
    first_scores, first_loads = evaluate(scores, loadings, observed, trial_mean, correlations, noise_var, plot_slot, row_count, col_count, panel_list, score_precision)
    new_scores = (scores.astype(jnp.float32) - 0.005 * first_scores).astype(jnp.bfloat16)
    new_loads = loadings - 0.02 * first_loads
    return evaluate(new_scores, new_loads, observed, trial_mean, correlations, noise_var, plot_slot, row_count, col_count, panel_list, score_precision)
```

```python
import functools

import jax
import jax.numpy as jnp
from jax import lax
from jax.experimental import pallas as pl
from jax.experimental.pallas import tpu as pltpu
from jax.sharding import PartitionSpec as P

PANEL = 128
TILE = 8

score_step = 0.005
load_step = 0.02

MESH = pl.DeviceIdType.MESH
F32 = jnp.float32
BF16 = jnp.bfloat16


def halves(x):
    high = x.astype(BF16).astype(F32)
    return high, x - high


def dot(a, b):
    return lax.dot_general(a, b, (((1,), (0,)), ((), ())), preferred_element_type=F32)


def dot_nt(a, b):
    return lax.dot_general(a, b, (((1,), (1,)), ((), ())), preferred_element_type=F32)


def kernel(
    n_trial,
    n_factor,
    rank_tile,
    mean_ref,
    corr_ref,
    noise_ref,
    rows_ref,
    cols_ref,
    observed_ref,
    slot_ref,
    scores_ref,
    loads_ref,
    precision_ref,
    source_ref,
    local_ref,
    place_ref,
    score_out,
    load_out,
    sent,
    got,
    fac_sent,
    fac_got,
    spread,
    cells,
    fresh,
    send_sem,
    recv_sem,
    fac_send_sem,
    fac_recv_sem,
):
    per_dev, grid_rows, grid_cols = observed_ref.shape
    factors = scores_ref.shape[0]
    owned = scores_ref.shape[1] // PANEL
    required = place_ref.shape[0]
    per_trial = required // per_dev
    rows = n_trial * rank_tile
    me = lax.axis_index("trial")
    mine = lax.axis_index("factor")

    barrier = pltpu.get_barrier_semaphore()
    for step in range(1, n_trial):
        pl.semaphore_signal(
            barrier,
            inc=1,
            device_id={"trial": lax.rem(me + step, n_trial)},
            device_id_type=MESH,
        )
    for step in range(1, n_factor):
        pl.semaphore_signal(
            barrier,
            inc=1,
            device_id={"factor": lax.rem(mine + step, n_factor)},
            device_id_type=MESH,
        )

    def tile_at(index):
        return pl.ds(pl.multiple_of(index * rank_tile, rank_tile), rank_tile)

    def send(number):
        got[number, tile_at(me), :] = sent[number, tile_at(me), :]
        for step in range(1, n_trial):
            target = lax.rem(me + step, n_trial)
            pltpu.make_async_remote_copy(
                src_ref=sent.at[number, tile_at(target)],
                dst_ref=got.at[number, tile_at(me)],
                send_sem=send_sem.at[number],
                recv_sem=recv_sem.at[number],
                device_id={"trial": target},
                device_id_type=MESH,
            ).start()

    def others(number, ref, sem):
        part = ref.at[number, pl.ds(0, (n_trial - 1) * rank_tile)]
        return pltpu.make_async_copy(part, part, sem.at[number])

    def receive(number):
        others(number, got, recv_sem).wait()
        return got[number]

    def factor_sum(number, part):
        fac_sent[number] = part
        fac_got[number, pl.ds(mine, 1)] = part[None]
        for step in range(1, n_factor):
            pltpu.make_async_remote_copy(
                src_ref=fac_sent.at[number],
                dst_ref=fac_got.at[number, mine],
                send_sem=fac_send_sem.at[number, step - 1],
                recv_sem=fac_recv_sem.at[number, step - 1],
                device_id={"factor": lax.rem(mine + step, n_factor)},
                device_id_type=MESH,
            ).start()
        for step in range(1, n_factor):
            origin = lax.rem(mine + n_factor - step, n_factor)
            pltpu.make_async_copy(
                fac_sent.at[number], fac_got.at[number, origin], fac_recv_sem.at[number, step - 1]
            ).wait()
        total = fac_got[number, 0]
        for index in range(1, n_factor):
            total = total + fac_got[number, index]
        return total

    source = source_ref[...]
    trial_of = jnp.where(source >= 0, source // per_trial, -1)
    local_of = local_ref[...]

    def load_rows(loads):
        total = jnp.zeros((rows, factors), F32)
        for trial in range(per_dev):
            total = jnp.where(trial_of == trial, loads[trial : trial + 1, :], total)
        return total

    loads = loads_ref[...]
    sent[0, :, :] = jnp.concatenate(
        [
            load_rows(loads),
            jnp.broadcast_to(local_of, (rows, PANEL - factors)),
        ],
        axis=1,
    )
    pl.semaphore_wait(barrier, n_trial - 1 + n_factor - 1)
    send(0)

    lane_rows = lax.broadcasted_iota(jnp.int32, (required, rows), 1)
    unpack = jnp.where(place_ref[...] == lane_rows, 1.0, 0.0).astype(BF16)
    unpack = jnp.concatenate([unpack, unpack], axis=1)
    lane_slots = lax.broadcasted_iota(jnp.int32, (rows, required), 1)
    pack = jnp.where(source == lane_slots, 1.0, 0.0)
    pack = jnp.concatenate([pack, pack], axis=1).astype(BF16)
    cell_iota = lax.broadcasted_iota(jnp.int32, (PANEL, grid_cols), 0)
    panel_iota = lax.broadcasted_iota(jnp.int32, (per_trial, grid_cols), 0)
    for trial in range(per_dev):
        cell = slot_ref[trial] & (PANEL - 1)
        for row in range(grid_rows):
            cells[trial, :, row * grid_cols : (row + 1) * grid_cols] = jnp.where(
                cell[row : row + 1, :] == cell_iota, 1.0, 0.0
            ).astype(BF16)

    row_index = lax.broadcasted_iota(jnp.int32, (grid_rows, grid_cols), 0)
    col_index = lax.broadcasted_iota(jnp.int32, (grid_rows, grid_cols), 1)

    def sweep(values, corr, position, limit, axis):
        length = values.shape[axis]
        scale = 1.0 / (1.0 - corr * corr)
        inner = jnp.where((position > 0) & (position < limit - 1), corr * corr, 0.0)
        lower = jnp.where(position == 0, 0.0, pltpu.roll(values, 1, axis))
        upper = jnp.where(position == length - 1, 0.0, pltpu.roll(values, length - 1, axis))
        result = scale * ((1.0 + inner) * values - corr * (lower + upper))
        return jnp.where(position < limit, result, 0.0)

    def plots(effect):
        totals = []
        for trial in range(per_dev):
            slot = slot_ref[trial]
            panel = slot // PANEL
            cell = slot & (PANEL - 1)
            fitted = jnp.zeros((grid_rows, grid_cols), F32)
            for index in range(per_trial):
                at = trial * per_trial + index
                line = jnp.broadcast_to(effect[at : at + 1, :], (grid_rows, PANEL))
                taken = jnp.take_along_axis(line, cell, axis=1)
                fitted = jnp.where(panel == index, taken, fitted)
            row_limit = rows_ref[trial]
            col_limit = cols_ref[trial]
            active = (row_index < row_limit) & (col_index < col_limit)
            residual = jnp.where(active, observed_ref[trial] - mean_ref[trial] - fitted, 0.0)
            row_corr = jnp.full((grid_rows, grid_cols), corr_ref[trial, 0], F32)
            col_corr = jnp.full((grid_rows, grid_cols), corr_ref[trial, 1], F32)
            noise = jnp.full((grid_rows, grid_cols), noise_ref[trial], F32)
            across = sweep(residual, col_corr, col_index, col_limit, 1)
            weighted = sweep(across, row_corr, row_index, row_limit, 0) / noise
            high, low = halves(weighted)
            for row in range(grid_rows):
                match = panel[row : row + 1, :] == panel_iota
                where_to = slice(row * grid_cols, (row + 1) * grid_cols)
                spread[trial, 0:per_trial, where_to] = jnp.where(
                    match, high[row : row + 1, :], 0.0
                ).astype(BF16)
                spread[trial, per_trial : 2 * per_trial, where_to] = jnp.where(
                    match, low[row : row + 1, :], 0.0
                ).astype(BF16)
            both = dot_nt(spread[trial], cells[trial])
            totals.append(both[0:per_trial] + both[per_trial : 2 * per_trial])
        return jnp.concatenate(totals, axis=0)

    def evaluate(first, load_part, panel_of, panel_lane, current_ref):
        load_high, load_low = halves(load_part)
        load_both = jnp.concatenate([load_high, load_low], axis=1).astype(BF16)
        effect = jnp.zeros((rows, PANEL), F32)
        for panel in range(owned):
            block = current_ref[:, panel * PANEL : (panel + 1) * PANEL]
            product = dot(load_both, jnp.concatenate([block, block], axis=0))
            effect = jnp.where(panel_of == panel, product, effect)
        sent[first] = effect
        send(first)
        arrived_high, arrived_low = halves(receive(first))
        table = dot(unpack, jnp.concatenate([arrived_high, arrived_low], axis=0).astype(BF16))
        slot_weight = plots(factor_sum(0 if first == 1 else 1, table))
        high, low = halves(slot_weight)
        sent[first + 1] = dot(pack, jnp.concatenate([high, low], axis=0).astype(BF16))
        send(first + 1)
        weight = receive(first + 1)
        high, low = halves(weight)
        weight_wide = jnp.concatenate([high, low], axis=1).astype(BF16)
        terms = jnp.zeros((rows, factors), F32)
        for panel in range(owned):
            block = current_ref[:, panel * PANEL : (panel + 1) * PANEL]
            product = dot_nt(weight_wide, jnp.concatenate([block, block], axis=1))
            terms = jnp.where(panel_of == panel, product, terms)
        sent[first + 2] = jnp.concatenate(
            [terms, jnp.zeros((rows, PANEL - factors), F32)], axis=1
        )
        send(first + 2)
        weight_tall = jnp.concatenate([high, low, high], axis=0).astype(BF16)
        lane_high, lane_low = halves(load_part_t(load_part))
        for panel in range(owned):
            where_to = slice(panel * PANEL, (panel + 1) * PANEL)
            match = panel_lane == panel
            masked_high = jnp.where(match, lane_high, 0.0)
            masked_low = jnp.where(match, lane_low, 0.0)
            left = jnp.concatenate([masked_high, masked_high, masked_low], axis=1).astype(BF16)
            current = current_ref[:, where_to].astype(F32)
            grad = precision_ref[...] * current - dot(left, weight_tall)
            if first == 1:
                fresh[:, where_to] = (current - score_step * grad).astype(BF16)
            else:
                score_out[:, where_to] = grad
        back = receive(first + 2)[:, 0:factors]
        sums = []
        for trial in range(per_dev):
            sums.append(
                jnp.sum(jnp.where(trial_of == trial, back, 0.0), axis=0, keepdims=True)
            )
        return jnp.concatenate(sums, axis=0)

    def load_part_t(load_part):
        wide = jnp.concatenate([load_part, jnp.zeros((rows, PANEL - factors), F32)], axis=1)
        return wide.T[0:factors, :]

    message = receive(0)
    panel_of = message[:, factors : factors + 1]
    panel_lane = message.T[factors : factors + 1, :]
    gained = evaluate(1, message[:, 0:factors], panel_of, panel_lane, scores_ref)
    new_loads = loads + load_step * gained
    sent[4] = jnp.concatenate(
        [load_rows(new_loads), jnp.zeros((rows, PANEL - factors), F32)], axis=1
    )
    send(4)
    gained = evaluate(5, receive(4)[:, 0:factors], panel_of, panel_lane, fresh)
    load_out[...] = -gained

    for number in range(8):
        others(number, sent, send_sem).wait()
    for number in range(2):
        for step in range(1, n_factor):
            pltpu.make_async_copy(
                fac_sent.at[number], fac_sent.at[number], fac_send_sem.at[number, step - 1]
            ).wait()


def body(
    observed,
    trial_mean,
    correlations,
    noise_var,
    plot_slot,
    row_count,
    col_count,
    panel_list,
    scores,
    loadings,
    score_precision,
):
    n_trial = lax.axis_size("trial")
    n_factor = lax.axis_size("factor")
    per_dev, per_trial = panel_list.shape
    required = per_dev * per_trial
    most = 2 * required // n_trial
    rank_tile = -(-most // TILE) * TILE
    rows = n_trial * rank_tile
    factors = scores.shape[0]
    owned = scores.shape[1] // PANEL
    wanted = panel_list.reshape(required)
    owner = wanted // owned
    local = wanted - owner * owned
    later = lax.broadcasted_iota(jnp.int32, (required, required), 0)
    other = lax.broadcasted_iota(jnp.int32, (required, required), 1)
    earlier = (owner[None, :] == owner[:, None]) & (other < later)
    place = owner * rank_tile + jnp.sum(earlier.astype(jnp.int32), axis=1)
    placed = place[None, :] == lax.broadcasted_iota(jnp.int32, (rows, required), 0)
    slots = lax.broadcasted_iota(jnp.int32, (rows, required), 1)
    source = jnp.max(jnp.where(placed, slots, -1), axis=1, keepdims=True)
    local_of = jnp.max(jnp.where(placed, local[None, :], -1), axis=1, keepdims=True)

    vmem = pl.BlockSpec(memory_space=pltpu.VMEM)
    smem = pl.BlockSpec(memory_space=pltpu.SMEM)
    grid_size = plot_slot.shape[1] * plot_slot.shape[2]
    return pl.pallas_call(
        functools.partial(kernel, n_trial, n_factor, rank_tile),
        out_shape=(
            jax.ShapeDtypeStruct(scores.shape, F32),
            jax.ShapeDtypeStruct(loadings.shape, F32),
        ),
        in_specs=[smem] * 5 + [vmem] * 8,
        out_specs=(vmem, vmem),
        scratch_shapes=[
            pltpu.VMEM((8, rows, PANEL), F32),
            pltpu.VMEM((8, rows, PANEL), F32),
            pltpu.VMEM((2, required, PANEL), F32),
            pltpu.VMEM((2, n_factor, required, PANEL), F32),
            pltpu.VMEM((per_dev, 2 * per_trial, grid_size), BF16),
            pltpu.VMEM((per_dev, PANEL, grid_size), BF16),
            pltpu.VMEM(scores.shape, BF16),
            pltpu.SemaphoreType.DMA((8,)),
            pltpu.SemaphoreType.DMA((8,)),
            pltpu.SemaphoreType.DMA((2, max(n_factor - 1, 1))),
            pltpu.SemaphoreType.DMA((2, max(n_factor - 1, 1))),
        ],
        compiler_params=pltpu.CompilerParams(
            collective_id=0, has_side_effects=True, vmem_limit_bytes=48 * 1024 * 1024
        ),
    )(
        trial_mean,
        correlations,
        noise_var,
        row_count,
        col_count,
        observed,
        plot_slot,
        scores,
        loadings,
        score_precision[:, None],
        source,
        local_of.astype(F32),
        place[:, None],
    )


def solution(mesh):
    in_specs = (
        P("trial", None, None),
        P("trial"),
        P("trial", None),
        P("trial"),
        P("trial", None, None),
        P("trial"),
        P("trial"),
        P("trial", None),
        P("factor", "trial"),
        P("trial", "factor"),
        P("factor"),
    )
    out_specs = (P("factor", "trial"), P("trial", "factor"))
    return jax.shard_map(body, mesh=mesh, in_specs=in_specs, out_specs=out_specs, check_vma=False)
```

```python
import functools

import jax
import jax.numpy as jnp
from jax import lax
from jax.experimental import pallas as pl
from jax.experimental.pallas import tpu as pltpu
from jax.sharding import PartitionSpec as P

PANEL = 128
TILE = 8

score_step = 0.005
load_step = 0.02

MESH = pl.DeviceIdType.MESH
F32 = jnp.float32
BF16 = jnp.bfloat16
LEVELS = 32000.0


def halves(x):
    high = x.astype(BF16).astype(F32)
    return high, x - high


def dot(a, b):
    return lax.dot_general(a, b, (((1,), (0,)), ((), ())), preferred_element_type=F32)


def dot_nt(a, b):
    return lax.dot_general(a, b, (((1,), (1,)), ((), ())), preferred_element_type=F32)


def kernel(
    n_trial,
    n_factor,
    rank_tile,
    mean_hbm,
    corr_hbm,
    noise_hbm,
    rows_hbm,
    cols_hbm,
    list_hbm,
    precision_hbm,
    loads_hbm,
    scores_hbm,
    slot_hbm,
    observed_hbm,
    score_out,
    load_out,
    mean_ref,
    corr_ref,
    noise_ref,
    rows_ref,
    cols_ref,
    list_ref,
    precision_ref,
    loads_ref,
    scores_ref,
    slot_ref,
    observed_ref,
    sent,
    got,
    share,
    shares,
    scale,
    scales,
    fac_sent,
    fac_got,
    spread,
    cells,
    fresh,
    copy_sem,
    send_sem,
    recv_sem,
    fac_send_sem,
    fac_recv_sem,
):
    per_dev, grid_rows, grid_cols = observed_ref.shape
    factors = scores_ref.shape[0]
    owned = scores_ref.shape[1] // PANEL
    per_trial = list_ref.shape[1]
    required = per_dev * per_trial
    rows = n_trial * rank_tile
    trials = n_trial * per_dev
    me = lax.axis_index("trial")
    mine = lax.axis_index("factor")

    barrier = pltpu.get_barrier_semaphore()
    for step in range(1, n_trial):
        pl.semaphore_signal(
            barrier,
            inc=1,
            device_id={"trial": lax.rem(me + step, n_trial)},
            device_id_type=MESH,
        )
    for step in range(1, n_factor):
        pl.semaphore_signal(
            barrier,
            inc=1,
            device_id={"factor": lax.rem(mine + step, n_factor)},
            device_id_type=MESH,
        )

    pairs = (
        (list_hbm, list_ref),
        (loads_hbm, loads_ref),
        (slot_hbm, slot_ref),
        (scores_hbm, scores_ref),
        (observed_hbm, observed_ref),
        (precision_hbm, precision_ref),
        (mean_hbm, mean_ref),
        (corr_hbm, corr_ref),
        (noise_hbm, noise_ref),
        (rows_hbm, rows_ref),
        (cols_hbm, cols_ref),
    )
    copies = [
        pltpu.make_async_copy(source, target, copy_sem.at[index])
        for index, (source, target) in enumerate(pairs)
    ]
    for copy in copies:
        copy.start()

    def tile_at(index):
        return pl.ds(pl.multiple_of(index * rank_tile, rank_tile), rank_tile)

    def send(number):
        for step in range(1, n_trial):
            target = lax.rem(me + step, n_trial)
            pltpu.make_async_remote_copy(
                src_ref=sent.at[number, tile_at(target)],
                dst_ref=got.at[number, tile_at(me)],
                send_sem=send_sem.at[number],
                recv_sem=recv_sem.at[number],
                device_id={"trial": target},
                device_id_type=MESH,
            ).start()
        got[number, tile_at(me), :] = sent[number, tile_at(me), :]

    def others(number, ref, sem):
        part = ref.at[number, pl.ds(0, (n_trial - 1) * rank_tile)]
        return pltpu.make_async_copy(part, part, sem.at[number])

    def receive(number):
        others(number, got, recv_sem).wait()
        return got[number]

    def send_share():
        for step in range(1, n_trial):
            pltpu.make_async_remote_copy(
                src_ref=share,
                dst_ref=shares.at[me],
                send_sem=send_sem.at[6],
                recv_sem=recv_sem.at[6],
                device_id={"trial": lax.rem(me + step, n_trial)},
                device_id_type=MESH,
            ).start()
            pltpu.make_async_remote_copy(
                src_ref=scale.at[pl.ds(0, 1)],
                dst_ref=scales.at[pl.ds(me, 1)],
                send_sem=send_sem.at[7],
                recv_sem=recv_sem.at[7],
                device_id={"trial": lax.rem(me + step, n_trial)},
                device_id_type=MESH,
            ).start()
        shares[pl.ds(me, 1)] = share[...][None]
        scales[pl.ds(me, 1), :] = scale[0:1, :]

    def other_shares(sem):
        part = shares.at[pl.ds(0, n_trial - 1)]
        return pltpu.make_async_copy(part, part, sem.at[6])

    def other_scales(sem):
        part = scales.at[pl.ds(0, n_trial - 1)]
        return pltpu.make_async_copy(part, part, sem.at[7])

    def factor_sum(number, part):
        fac_sent[number] = part
        for step in range(1, n_factor):
            pltpu.make_async_remote_copy(
                src_ref=fac_sent.at[number],
                dst_ref=fac_got.at[number, mine],
                send_sem=fac_send_sem.at[number, step - 1],
                recv_sem=fac_recv_sem.at[number, step - 1],
                device_id={"factor": lax.rem(mine + step, n_factor)},
                device_id_type=MESH,
            ).start()
        fac_got[number, pl.ds(mine, 1)] = part[None]
        for step in range(1, n_factor):
            origin = lax.rem(mine + n_factor - step, n_factor)
            pltpu.make_async_copy(
                fac_sent.at[number], fac_got.at[number, origin], fac_recv_sem.at[number, step - 1]
            ).wait()
        total = fac_got[number, 0]
        for index in range(1, n_factor):
            total = total + fac_got[number, index]
        return total

    def column(line):
        size = line.shape[1]
        eye = lax.broadcasted_iota(jnp.int32, (size, size), 0) == lax.broadcasted_iota(
            jnp.int32, (size, size), 1
        )
        return jnp.sum(jnp.where(eye, line, 0.0), axis=1, keepdims=True)

    copies[0].wait()
    wanted = jnp.concatenate(
        [list_ref[trial : trial + 1, :] for trial in range(per_dev)], axis=1
    )
    owner = wanted // owned
    local = wanted - owner * owned
    owner_line = owner.astype(F32)
    before = lax.broadcasted_iota(jnp.int32, (required, required), 0)
    after = lax.broadcasted_iota(jnp.int32, (required, required), 1)
    earlier = (column(owner_line) == owner_line) & (before < after)
    rank = jnp.sum(jnp.where(earlier, 1.0, 0.0), axis=0, keepdims=True)
    place = owner_line * rank_tile + rank
    row_of = lax.broadcasted_iota(jnp.int32, (rows, required), 0).astype(F32)
    placed = place == row_of
    slot_trial = lax.broadcasted_iota(jnp.int32, (rows, required), 1) // per_trial
    trial_of = jnp.max(jnp.where(placed, slot_trial.astype(F32), -1.0), axis=1, keepdims=True)
    local_of = jnp.max(jnp.where(placed, local.astype(F32), -1.0), axis=1, keepdims=True)
    pack = jnp.where(placed, 1.0, 0.0)
    pack = jnp.concatenate([pack, pack], axis=1).astype(BF16)

    copies[1].wait()
    loads = loads_ref[...]
    load_rows = jnp.zeros((rows, factors), F32)
    for trial in range(per_dev):
        load_rows = jnp.where(trial_of == trial, loads[trial : trial + 1, :], load_rows)
    sent[0] = jnp.concatenate(
        [
            load_rows,
            jnp.broadcast_to(local_of, (rows, 8)),
            jnp.broadcast_to(trial_of, (rows, PANEL - factors - 8)),
        ],
        axis=1,
    )
    pl.semaphore_wait(barrier, n_trial - 1 + n_factor - 1)
    send(0)

    lane_rows = lax.broadcasted_iota(jnp.int32, (required, rows), 1).astype(F32)
    unpack = jnp.where(column(place) == lane_rows, 1.0, 0.0).astype(BF16)
    unpack = jnp.concatenate([unpack, unpack], axis=1)
    cell_iota = lax.broadcasted_iota(jnp.int32, (PANEL, grid_cols), 0)
    panel_iota = lax.broadcasted_iota(jnp.int32, (per_trial, grid_cols), 0)
    for copy in copies[2:]:
        copy.wait()
    precision = column(precision_ref[...])
    for trial in range(per_dev):
        cell = slot_ref[trial] & (PANEL - 1)
        for row in range(grid_rows):
            cells[trial, :, row * grid_cols : (row + 1) * grid_cols] = jnp.where(
                cell[row : row + 1, :] == cell_iota, 1.0, 0.0
            ).astype(BF16)

    row_index = lax.broadcasted_iota(jnp.int32, (grid_rows, grid_cols), 0)
    col_index = lax.broadcasted_iota(jnp.int32, (grid_rows, grid_cols), 1)

    def sweep(values, corr, position, limit, axis):
        length = values.shape[axis]
        scale = 1.0 / (1.0 - corr * corr)
        inner = jnp.where((position > 0) & (position < limit - 1), corr * corr, 0.0)
        lower = jnp.where(position == 0, 0.0, pltpu.roll(values, 1, axis))
        upper = jnp.where(position == length - 1, 0.0, pltpu.roll(values, length - 1, axis))
        result = scale * ((1.0 + inner) * values - corr * (lower + upper))
        return jnp.where(position < limit, result, 0.0)

    def over_grid(ref, row, lane):
        return jnp.broadcast_to(ref[row : row + 1, lane : lane + 1], (grid_rows, grid_cols))

    def plots(effect):
        totals = []
        for trial in range(per_dev):
            slot = slot_ref[trial]
            panel = slot // PANEL
            cell = slot & (PANEL - 1)
            fitted = jnp.zeros((grid_rows, grid_cols), F32)
            for index in range(per_trial):
                at = trial * per_trial + index
                line = jnp.broadcast_to(effect[at : at + 1, :], (grid_rows, PANEL))
                taken = jnp.take_along_axis(line, cell, axis=1)
                fitted = jnp.where(panel == index, taken, fitted)
            row_limit = over_grid(rows_ref, 0, trial)
            col_limit = over_grid(cols_ref, 0, trial)
            active = (row_index < row_limit) & (col_index < col_limit)
            residual = jnp.where(
                active, observed_ref[trial] - over_grid(mean_ref, 0, trial) - fitted, 0.0
            )
            across = sweep(residual, over_grid(corr_ref, trial, 1), col_index, col_limit, 1)
            weighted = sweep(across, over_grid(corr_ref, trial, 0), row_index, row_limit, 0)
            weighted = weighted / over_grid(noise_ref, 0, trial)
            high, low = halves(weighted)
            for row in range(grid_rows):
                match = panel[row : row + 1, :] == panel_iota
                where_to = slice(row * grid_cols, (row + 1) * grid_cols)
                spread[trial, 0:per_trial, where_to] = jnp.where(
                    match, high[row : row + 1, :], 0.0
                ).astype(BF16)
                spread[trial, per_trial : 2 * per_trial, where_to] = jnp.where(
                    match, low[row : row + 1, :], 0.0
                ).astype(BF16)
            both = dot_nt(spread[trial], cells[trial])
            totals.append(both[0:per_trial] + both[per_trial : 2 * per_trial])
        return jnp.concatenate(totals, axis=0)

    message = receive(0)
    first_loads = message[:, 0:factors]
    panel_of = message[:, factors : factors + 1]
    turned = message.T
    panel_lane = turned[factors : factors + 1, :]
    block_at = lax.broadcasted_iota(jnp.int32, (rows, 1), 0) // rank_tile * per_dev
    block_lane = lax.broadcasted_iota(jnp.int32, (1, rows), 1) // rank_tile * per_dev
    within = message[:, factors + 8 : factors + 9]
    within_lane = turned[factors + 8 : factors + 9, :]
    whose = jnp.where(within >= 0.0, within + block_at.astype(F32), -1.0)
    whose_lane = jnp.where(within_lane >= 0.0, within_lane + block_lane.astype(F32), -1.0)
    gather = whose == lax.broadcasted_iota(jnp.int32, (rows, trials), 1).astype(F32)
    gather = jnp.where(gather, 1.0, 0.0)
    gather = jnp.concatenate([gather, gather], axis=1).astype(BF16)
    collect = whose_lane == lax.broadcasted_iota(jnp.int32, (trials, rows), 0).astype(F32)
    collect = jnp.where(collect, 1.0, 0.0).astype(BF16)
    collect = jnp.concatenate([collect, collect], axis=1)

    def stacked(values):
        high, low = halves(values)
        return jnp.concatenate([high, low], axis=0).astype(BF16)

    def weigh(number, load_part, current_ref):
        load_high, load_low = halves(load_part)
        load_both = jnp.concatenate([load_high, load_low], axis=1).astype(BF16)
        effect = jnp.zeros((rows, PANEL), F32)
        for panel in range(owned):
            block = current_ref[:, panel * PANEL : (panel + 1) * PANEL]
            product = dot(load_both, jnp.concatenate([block, block], axis=0))
            effect = jnp.where(panel_of == panel, product, effect)
        sent[number] = effect
        send(number)
        table = dot(unpack, stacked(receive(number)))
        slot_weight = plots(factor_sum(0 if number == 1 else 1, table))
        sent[number + 1] = dot(pack, stacked(slot_weight))
        send(number + 1)
        return halves(receive(number + 1))

    def load_terms(high, low, current_ref):
        wide = jnp.concatenate([high, low], axis=1).astype(BF16)
        terms = jnp.zeros((rows, factors), F32)
        for panel in range(owned):
            block = current_ref[:, panel * PANEL : (panel + 1) * PANEL]
            product = dot_nt(wide, jnp.concatenate([block, block], axis=1))
            terms = jnp.where(panel_of == panel, product, terms)
        return terms

    def score_grads(high, low, load_lanes, current_ref):
        tall = jnp.concatenate([high, low, high], axis=0).astype(BF16)
        lane_high, lane_low = halves(load_lanes)
        for panel in range(owned):
            where_to = slice(panel * PANEL, (panel + 1) * PANEL)
            match = panel_lane == panel
            masked_high = jnp.where(match, lane_high, 0.0)
            masked_low = jnp.where(match, lane_low, 0.0)
            left = jnp.concatenate([masked_high, masked_high, masked_low], axis=1).astype(BF16)
            current = current_ref[:, where_to].astype(F32)
            yield where_to, current, precision * current - dot(left, tall)

    padding = jnp.zeros((rows, PANEL - factors), F32)
    high, low = weigh(1, first_loads, scores_ref)
    partial = dot(collect, stacked(load_terms(high, low, scores_ref)))
    groups = PANEL // factors
    depth = trials // groups
    packed = jnp.concatenate(
        [partial[index * depth : (index + 1) * depth] for index in range(groups)], axis=1
    )
    unit = jnp.max(jnp.abs(packed), axis=1, keepdims=True) * (1.0 / LEVELS) + 1e-30
    share[...] = jnp.floor(packed / unit + 0.5).astype(jnp.int32).astype(jnp.int16)
    square = jnp.concatenate(
        [jnp.broadcast_to(unit, (depth, PANEL)), jnp.zeros((PANEL - depth, PANEL), F32)], axis=0
    )
    scale[...] = square.T[0:TILE, :]
    send_share()
    for where_to, current, grad in score_grads(high, low, turned[0:factors, :], scores_ref):
        fresh[:, where_to] = (current - score_step * grad).astype(BF16)
    other_shares(recv_sem).wait()
    other_scales(recv_sem).wait()
    tall_scales = scales[...]
    if n_trial < PANEL:
        tall_scales = jnp.concatenate(
            [tall_scales, jnp.zeros((PANEL - n_trial, PANEL), F32)], axis=0
        )
    units = tall_scales.T[0:depth, :]
    summed = jnp.zeros((depth, PANEL), F32)
    for index in range(n_trial):
        whole = shares[index].astype(jnp.int32).astype(F32)
        summed = summed + whole * units[:, index : index + 1]
    gained = jnp.concatenate(
        [summed[:, index * factors : (index + 1) * factors] for index in range(groups)], axis=0
    )
    second_loads = first_loads + load_step * dot(gather, stacked(gained))
    high, low = weigh(3, second_loads, fresh)
    sent[5] = jnp.concatenate([load_terms(high, low, fresh), padding], axis=1)
    send(5)
    turned_loads = jnp.concatenate([second_loads, padding], axis=1).T[0:factors, :]
    for where_to, current, grad in score_grads(high, low, turned_loads, fresh):
        score_out[:, where_to] = grad
    back = receive(5)[:, 0:factors]
    for trial in range(per_dev):
        load_out[trial : trial + 1, :] = -jnp.sum(
            jnp.where(trial_of == trial, back, 0.0), axis=0, keepdims=True
        )

    for number in range(6):
        others(number, sent, send_sem).wait()
    other_shares(send_sem).wait()
    other_scales(send_sem).wait()
    for number in range(2):
        for step in range(1, n_factor):
            pltpu.make_async_copy(
                fac_sent.at[number], fac_sent.at[number], fac_send_sem.at[number, step - 1]
            ).wait()


def body(
    observed,
    trial_mean,
    correlations,
    noise_var,
    plot_slot,
    row_count,
    col_count,
    panel_list,
    scores,
    loadings,
    score_precision,
):
    n_trial = lax.axis_size("trial")
    n_factor = lax.axis_size("factor")
    per_dev, per_trial = panel_list.shape
    required = per_dev * per_trial
    most = 2 * required // n_trial
    rank_tile = -(-most // TILE) * TILE
    rows = n_trial * rank_tile
    factors = scores.shape[0]
    depth = n_trial * per_dev * factors // PANEL
    grid_size = plot_slot.shape[1] * plot_slot.shape[2]
    operands = (
        trial_mean[None],
        correlations,
        noise_var[None],
        row_count[None],
        col_count[None],
        panel_list,
        score_precision[None],
        loadings,
        scores,
        plot_slot,
        observed,
    )
    vmem = pl.BlockSpec(memory_space=pltpu.VMEM)
    hbm = pl.BlockSpec(memory_space=pltpu.HBM)
    return pl.pallas_call(
        functools.partial(kernel, n_trial, n_factor, rank_tile),
        out_shape=(
            jax.ShapeDtypeStruct(scores.shape, F32),
            jax.ShapeDtypeStruct(loadings.shape, F32),
        ),
        in_specs=[hbm] * len(operands),
        out_specs=(vmem, vmem),
        scratch_shapes=[pltpu.VMEM(operand.shape, operand.dtype) for operand in operands]
        + [
            pltpu.VMEM((6, rows, PANEL), F32),
            pltpu.VMEM((6, rows, PANEL), F32),
            pltpu.VMEM((depth, PANEL), jnp.int16),
            pltpu.VMEM((n_trial, depth, PANEL), jnp.int16),
            pltpu.VMEM((TILE, PANEL), F32),
            pltpu.VMEM((n_trial, PANEL), F32),
            pltpu.VMEM((2, required, PANEL), F32),
            pltpu.VMEM((2, n_factor, required, PANEL), F32),
            pltpu.VMEM((per_dev, 2 * per_trial, grid_size), BF16),
            pltpu.VMEM((per_dev, PANEL, grid_size), BF16),
            pltpu.VMEM(scores.shape, BF16),
            pltpu.SemaphoreType.DMA((len(operands),)),
            pltpu.SemaphoreType.DMA((8,)),
            pltpu.SemaphoreType.DMA((8,)),
            pltpu.SemaphoreType.DMA((2, max(n_factor - 1, 1))),
            pltpu.SemaphoreType.DMA((2, max(n_factor - 1, 1))),
        ],
        compiler_params=pltpu.CompilerParams(
            collective_id=0, has_side_effects=True, vmem_limit_bytes=48 * 1024 * 1024
        ),
    )(*operands)


def solution(mesh):
    in_specs = (
        P("trial", None, None),
        P("trial"),
        P("trial", None),
        P("trial"),
        P("trial", None, None),
        P("trial"),
        P("trial"),
        P("trial", None),
        P("factor", "trial"),
        P("trial", "factor"),
        P("factor"),
    )
    out_specs = (P("factor", "trial"), P("trial", "factor"))
    return jax.shard_map(body, mesh=mesh, in_specs=in_specs, out_specs=out_specs, check_vma=False)
```
